32 devices in a mesh: gx: 2 (over z_hi), gy: 2 (over z_lo), gz: 8 (over y, x, core).
Axes of the slice: x: 2, y: 2, z: 4 (z_hi: 2, z_lo: 2; z = z_hi * 2 + z_lo), core: 2. Of those that a mesh axis runs over, the one named last changes fastest.
Arguments:
- amplitudes: float32 [2, 8388608], P(None, ('gx', 'gy', 'gz')), may hold values from -6 to 6
- gates: float32 [6, 2, 128, 128], replicated, may hold values from -0.375 to 0.375
- gate_wires: int32 [6, 7], replicated, may hold values from 0 to 6, each once within a row
Outputs:
- evolved: float32 [2, 8388608], P(None, ('gx', 'gy', 'gz'))
The draws below stay inside these ranges and needn't reach their ends.
Inputs may be any that keep to these rules, and one draw needn't show every extreme that they name: Each row of gate_wires is an ordering of the numbers below 7.
All inputs are finite; a program needn't handle non-finite values.
Results may differ from the reference program's by a relative error of at most 0.00007.
Values sent between devices are 32-bit elements; how exact they have to be, the bound alone decides.
No kernel may reach another device: no remote copies, remote signals or barrier semaphores. Data moves between devices by JAX's collectives and lax.ppermute only.
A program may use at most 64 MiB of HBM per device.

```python
import jax
import jax.numpy as jnp
from jax import lax

LOCAL = 262144
GATE = 128
WINDOW = 7
GATES = 6
AMPS = 8388608
N_GX = 2
N_GY = 2
N_GZ = 8


def level_of(own_key, dims, cuts, smallest, high):
    def one(position, blocks):
        steps = jax.random.uniform(jax.random.fold_in(jax.random.fold_in(own_key, 6), position), (blocks,), jnp.float32, smallest / len(cuts), high / len(cuts))
        return jnp.repeat(jnp.exp(steps), dims[position] // blocks).reshape((-1,) + (1,) * (len(dims) - position - 1))

    loudness = one(*cuts[0])
    for cut in cuts[1:]:
        loudness = loudness * one(*cut)
    return loudness


def gaussian(own_key, dims, width, reach, split=(), kind=jnp.bfloat16):
    level = level_of(own_key, dims, split, -0.22, 0.18) if split else 1.0
    drawn = jax.random.normal(own_key, dims, jnp.float32) * width * level
    return jnp.minimum(jnp.maximum(drawn, -reach), reach).astype(kind)


def setup_inputs(seed: int = 0) -> dict:
    key_of = jax.random.split(jax.random.key(seed), 4)
    return {
        "amplitudes": gaussian(key_of[0], (2, AMPS), 1.0, 6.0, ((1, 32),), jnp.float32),
        "gates": gaussian(key_of[1], (GATES, 2, GATE, GATE), (2 * GATE) ** -0.5, 0.375, (), jnp.float32),
        "gate_wires": jax.vmap(lambda own: jax.random.permutation(own, WINDOW))(jax.random.split(key_of[2], GATES)).reshape((GATES, WINDOW)).astype(jnp.int32),
    }


def window_matrix(gate_pair, wire_list):
    gate_order = gate_pair.shape[-1]
    positions = jnp.arange(gate_order, dtype=jnp.int32)
    digits = jnp.arange(wire_list.shape[0], dtype=jnp.int32)
    digit_bits = jnp.right_shift(positions[:, None], digits[None, :]) & 1
    mapped = jnp.sum(jnp.left_shift(digit_bits, wire_list[None, :]), axis=1).astype(jnp.int32)
    return gate_pair[:, mapped][:, :, mapped]


def product(matrix, shaped):
    return jnp.einsum("wv,avb->awb", matrix, shaped, precision=lax.Precision.HIGHEST)


def apply_gate(vector, matrix, stride):
    count = vector.shape[1]
    gate_order = matrix.shape[-1]
    shaped = vector.reshape(2, count // (gate_order * stride), gate_order, stride)
    real_part = product(matrix[0], shaped[0]) - product(matrix[1], shaped[1])
    imag_part = product(matrix[0], shaped[1]) + product(matrix[1], shaped[0])
    return jnp.stack([real_part, imag_part]).reshape(2, count)


def reference(amplitudes, gates, gate_wires):
    windows = [window_matrix(gates[g], gate_wires[g]) for g in range(GATES)]
    top_stride = LOCAL // GATE
    mid_stride = min(GATE, LOCAL // GATE)
    group = N_GY * N_GZ
    vector = amplitudes.reshape(2, N_GX, group, group, LOCAL // group)
    vector = jnp.transpose(vector, (0, 1, 3, 2, 4)).reshape(2, AMPS)
    vector = apply_gate(vector, windows[0], 1)
    vector = apply_gate(vector, windows[1], top_stride)
    vector = vector.reshape(2, N_GX, group, N_GX, LOCAL // N_GX)
    vector = jnp.transpose(vector, (0, 3, 2, 1, 4)).reshape(2, AMPS)
    vector = apply_gate(vector, windows[2], mid_stride)
    vector = apply_gate(vector, windows[3], top_stride)
    vector = vector.reshape(2, N_GX * N_GY, N_GZ, N_GZ, LOCAL // N_GZ)
    vector = jnp.transpose(vector, (0, 1, 3, 2, 4)).reshape(2, AMPS)
    vector = apply_gate(vector, windows[4], 1)
    vector = apply_gate(vector, windows[5], top_stride)
    return vector
```

```python
import functools

import jax
import jax.numpy as jnp
from jax import lax
from jax.experimental import pallas as pl
from jax.experimental.pallas import tpu as pltpu
from jax.sharding import PartitionSpec as P

F32 = jnp.float32
BF16 = jnp.bfloat16
VMEM = pl.BlockSpec(memory_space=pltpu.VMEM)
SMEM = pl.BlockSpec(memory_space=pltpu.SMEM)


def bits_of(size):
    count = size.bit_length() - 1
    assert size == 1 << count
    return count


def halves(value):
    high = value.astype(BF16)
    return high, (value - high.astype(F32)).astype(BF16)


def dot(a, b):
    return jnp.dot(a, b, preferred_element_type=F32)


def product(left, right):
    return dot(left[0], right[0]) + (dot(left[0], right[1]) + dot(left[1], right[0]))


def complex_form(real, imag):
    return jnp.concatenate(
        [jnp.concatenate([real, -imag], axis=1), jnp.concatenate([imag, real], axis=1)], axis=0
    )


def row_form(real, imag):
    return jnp.concatenate(
        [jnp.concatenate([real, imag], axis=1), jnp.concatenate([-imag, real], axis=1)], axis=0
    )


def matrices_kernel(wires, flips, gates, lane_out, *left_outs):
    order = gates.shape[-1]
    width = wires.shape[1]
    rows = lax.broadcasted_iota(jnp.int32, (order, order), 0)
    columns = lax.broadcasted_iota(jnp.int32, (order, order), 1)

    def picker(g, flip):
        index = jnp.bitwise_xor(rows, flip)
        mapped = jnp.zeros_like(index)
        for j in range(width):
            bit = jnp.bitwise_and(jnp.right_shift(index, j), 1)
            mapped = mapped + jnp.left_shift(bit, wires[g, j])
        return jnp.where(mapped == columns, 1.0, 0.0).astype(BF16)

    def window(g, transposed):
        row_pick = picker(g, flips[g, 0])
        column_pick = picker(g, flips[g, 1])
        parts = []
        for c in range(2):
            pair = []
            for half in halves(gates[g, c]):
                first = dot(row_pick, half).astype(BF16)
                a, b = (column_pick, first) if transposed else (first, column_pick)
                pair.append(
                    lax.dot_general(a, b, (((1,), (1,)), ((), ())), preferred_element_type=F32)
                )
            parts.append(pair)
        return parts

    first, last = window(0, True), window(4, True)
    a = [jnp.concatenate([first[0][h], first[1][h]], axis=1).astype(BF16) for h in range(2)]
    b = [row_form(last[0][h], last[1][h]).astype(BF16) for h in range(2)]
    both = product(a, b)
    lane = halves(row_form(both[:, :order], both[:, order:]))
    lane_out[0] = lane[0]
    lane_out[1] = lane[1]
    for out, g in zip(left_outs, (1, 2, 3, 5)):
        parts = window(g, False)
        for h in range(2):
            out[h] = complex_form(parts[0][h], parts[1][h]).astype(BF16)


def matrices(gates, wires, flips):
    order = gates.shape[-1]
    shape = jax.ShapeDtypeStruct((2, 2 * order, 2 * order), BF16)
    return pl.pallas_call(
        matrices_kernel,
        out_shape=[shape] * 5,
        in_specs=[SMEM, SMEM, VMEM],
        out_specs=[VMEM] * 5,
        name="matrices",
    )(wires, flips, gates)


def runs(slots):
    merged = []
    for at, (operand, index) in enumerate(slots):
        if merged and merged[-1][0] == operand and merged[-1][1] + merged[-1][3] == index:
            merged[-1][3] += 1
        else:
            merged.append([operand, index, at, 1])
    return merged


def load_top(refs, slots, order, chunk, m, part):
    height = order // len(slots)
    step = 2 * chunk
    pieces = [
        refs[o][pl.ds(i * height * step + 2 * m + part, n * height, stride=step), :]
        for o, i, _, n in runs(slots)
    ]
    return pieces[0] if len(pieces) == 1 else jnp.concatenate(pieces, axis=0)


def store_top(refs, slots, order, chunk, m, part, value):
    height = order // len(slots)
    step = 2 * chunk
    for o, i, at, n in runs(slots):
        refs[o][pl.ds(i * height * step + 2 * m + part, n * height, stride=step), :] = value[
            at * height : (at + n) * height
        ]


def left(matrix, loads):
    columns = jnp.concatenate([jnp.concatenate(pair, axis=0) for pair in loads], axis=1)
    out = product((matrix[0], matrix[1]), halves(columns))
    order = matrix.shape[-1] // 2
    return [
        (out[:order, k * order : (k + 1) * order], out[order:, k * order : (k + 1) * order])
        for k in range(len(loads))
    ]


def top_gate(matrix, lane, order, chunk, sources, in_slots, targets, out_slots):
    per = min(2, chunk)

    def body(i, carry):
        ms = [per * i + k for k in range(per)]
        loads = [
            tuple(load_top(sources, in_slots, order, chunk, m, part) for part in range(2))
            for m in ms
        ]
        done = left(matrix, loads)
        if lane is not None:
            rows = jnp.concatenate([jnp.concatenate(pair, axis=1) for pair in done], axis=0)
            rows = product(halves(rows), (lane[0], lane[1]))
            done = [
                (rows[k * order : (k + 1) * order, :order], rows[k * order : (k + 1) * order, order:])
                for k in range(per)
            ]
        for m, pair in zip(ms, done):
            for part in range(2):
                store_top(targets, out_slots, order, chunk, m, part, pair[part])
        return carry

    lax.fori_loop(0, chunk // per, body, 0)


def inner_gate(matrix, order, middle, sources, slots, target):
    span = 2 * order
    blocks = order * middle // order
    per_slot = blocks // len(slots)
    for o, i, at, n in runs(slots):
        first, count = i * per_slot, n * per_slot
        base = at * per_slot

        def body(k, carry, o=o, first=first, base=base):
            loads = []
            for q in range(2):
                start = pl.multiple_of((first + 2 * k + q) * span, span)
                loads.append(
                    tuple(sources[o][pl.ds(start + part, order, stride=2), :] for part in range(2))
                )
            for q, pair in enumerate(left(matrix, loads)):
                start = pl.multiple_of((base + 2 * k + q) * span, span)
                for part in range(2):
                    target[pl.ds(start + part, order, stride=2), :] = pair[part]
            return carry

        lax.fori_loop(0, count // 2, body, 0)


def first_kernel(order, chunk, in_slots, out_slots, n_in, matrix, lane, *refs):
    top_gate(matrix, lane, order, chunk, refs[:n_in], in_slots, refs[n_in:], out_slots)


def middle_kernel(order, middle, in_slots, out_slots, n_in, inner, matrix, *refs):
    sources, targets, scratch = refs[:n_in], refs[n_in:-1], refs[-1]
    inner_gate(inner, order, middle, sources, in_slots, scratch)
    top_gate(matrix, None, order, middle, [scratch], [(0, 0)], targets, out_slots)


def last_kernel(order, chunk, in_slots, out_slots, n_in, matrix, *refs):
    top_gate(matrix, None, order, chunk, refs[:n_in], in_slots, refs[n_in:], out_slots)


def call(kernel, name, mats, sources, out_rows, lanes, scratch=()):
    return pl.pallas_call(
        kernel,
        out_shape=[jax.ShapeDtypeStruct((rows, lanes), F32) for rows in out_rows],
        in_specs=[VMEM] * (len(mats) + len(sources)),
        out_specs=[VMEM] * len(out_rows),
        scratch_shapes=list(scratch),
        name=name,
    )(*mats, *sources)


def swap(slots, arrays, height, axis, bit, index_bit):
    size = lax.axis_size(axis)
    pairs = [(i, i ^ (1 << bit)) for i in range(size)]
    leaving = [s for s in range(len(slots)) if s >> index_bit & 1]
    parts = [
        arrays[o][i * height : (i + n) * height] for o, i, _, n in runs([slots[s] for s in leaving])
    ]
    send = parts[0] if len(parts) == 1 else jnp.concatenate(parts, axis=0)
    got = lax.ppermute(send, axis, pairs)
    slots, arrays = list(slots), list(arrays) + [got]
    for at, s in enumerate(leaving):
        slots[s] = (len(arrays) - 1, at)
    return slots, arrays


def shards(amplitudes, gates, gate_wires):
    count = amplitudes.shape[1]
    order = gates.shape[-1]
    middle = count // (order * order)
    rows = 2 * count // order
    nx = bits_of(lax.axis_size("gx"))
    top = bits_of(order)
    group = lax.axis_size("gy") * lax.axis_size("gz")
    depth = lax.axis_size("gz")

    flip_x = jnp.left_shift(lax.axis_index("gx"), top - nx)
    zero = jnp.zeros_like(flip_x)
    flips = jnp.stack([zero, zero, flip_x, zero, zero, zero, zero, flip_x, zero, zero, zero, zero])
    lane, m1, m2, m3, m5 = matrices(gates, gate_wires, flips.reshape(6, 2))

    state = amplitudes.reshape(2, count // order, order).transpose(1, 0, 2).reshape(group, rows // group, order)
    state = lax.all_to_all(state, ("gy", "gz"), split_axis=0, concat_axis=0, tiled=True).reshape(rows, order)

    across = 1 << nx
    half = across // 2
    slots = [(s // half, s % half) for s in range(across)]
    arrays = call(
        functools.partial(first_kernel, order, middle, [(0, 0)], slots, 1),
        "first", (m1, lane), [state], [rows // 2] * 2, order,
    )
    for bit in reversed(range(nx)):
        slots, arrays = swap(slots, arrays, rows // across, "gx", bit, bit)
    used = sorted({s[0] for s in slots})
    slots = [(used.index(o), i) for o, i in slots]
    state = call(
        functools.partial(middle_kernel, order, middle, slots, [(0, 0)], len(used)),
        "middle", (m2, m3), [arrays[o] for o in used], [rows], order,
        [pltpu.VMEM((rows, order), F32)],
    )[0]
    state = state.reshape(depth, rows // depth, order)
    state = lax.all_to_all(state, "gz", split_axis=0, concat_axis=0, tiled=True).reshape(rows, order)
    state = call(
        functools.partial(last_kernel, order, middle, [(0, 0)], [(0, 0)], 1),
        "last", (m5,), [state], [rows], order,
    )[0]
    return state.reshape(count // order, 2, order).transpose(1, 0, 2).reshape(2, count)


def solution(mesh):
    in_specs = (P(None, ("gx", "gy", "gz")), P(), P())
    out_specs = P(None, ("gx", "gy", "gz"))
    return jax.shard_map(shards, mesh=mesh, in_specs=in_specs, out_specs=out_specs, check_vma=False)
```

```python
import functools

import jax
import jax.numpy as jnp
from jax import lax
from jax.experimental import pallas as pl
from jax.experimental.pallas import tpu as pltpu
from jax.experimental.layout import Layout, with_layout_constraint
from jax.sharding import PartitionSpec as P

F32 = jnp.float32
BF16 = jnp.bfloat16
VMEM = pl.BlockSpec(memory_space=pltpu.VMEM)
ANY = pl.BlockSpec(memory_space=pl.ANY)
LIMIT = pltpu.CompilerParams(vmem_limit_bytes=20 << 20)
SMEM = pl.BlockSpec(memory_space=pltpu.SMEM)


def bits_of(size):
    count = size.bit_length() - 1
    assert size == 1 << count
    return count


def in_vmem(shape):
    return pltpu.VMEM(shape.shape, shape.dtype)


def keep(value):
    return pltpu.with_memory_space_constraint(value, pltpu.VMEM)


def halves(value):
    high = value.astype(BF16)
    return high, (value - high.astype(F32)).astype(BF16)


def dot(a, b):
    return jnp.dot(a, b, preferred_element_type=F32)


def product(left, right):
    return dot(left[0], right[0]) + (dot(left[0], right[1]) + dot(left[1], right[0]))


def complex_form(real, imag):
    return jnp.concatenate(
        [jnp.concatenate([real, -imag], axis=1), jnp.concatenate([imag, real], axis=1)], axis=0
    )


def row_form(real, imag):
    return jnp.concatenate(
        [jnp.concatenate([real, imag], axis=1), jnp.concatenate([-imag, real], axis=1)], axis=0
    )


def matrices_kernel(middle, chunks, wires, flips, gates, lane_out, *left_outs):
    order = gates.shape[-1]
    width = wires.shape[1]
    rows = lax.broadcasted_iota(jnp.int32, (order, order), 0)
    columns = lax.broadcasted_iota(jnp.int32, (order, order), 1)

    def picker(g, flip):
        index = jnp.bitwise_xor(rows, flip)
        if g == 2:
            rest = bits_of(middle // chunks)
            low = bits_of(order // middle)
            index = (
                jnp.left_shift(jnp.bitwise_and(jnp.right_shift(rows, rest), (1 << low) - 1), bits_of(middle))
                + jnp.left_shift(jnp.right_shift(rows, rest + low), rest)
                + jnp.bitwise_and(rows, (1 << rest) - 1)
            )
        mapped = jnp.zeros_like(index)
        for j in range(width):
            bit = jnp.bitwise_and(jnp.right_shift(index, j), 1)
            mapped = mapped + jnp.left_shift(bit, wires[g, j])
        return jnp.where(mapped == columns, 1.0, 0.0).astype(BF16)

    def window(g, transposed):
        row_pick = picker(g, flips[g, 0])
        column_pick = picker(g, flips[g, 1])
        parts = []
        for c in range(2):
            pair = []
            for half in halves(gates[g, c]):
                first = dot(row_pick, half).astype(BF16)
                a, b = (column_pick, first) if transposed else (first, column_pick)
                pair.append(
                    lax.dot_general(a, b, (((1,), (1,)), ((), ())), preferred_element_type=F32)
                )
            parts.append(pair)
        return parts

    first, last = window(0, True), window(4, True)
    a = [jnp.concatenate([first[0][h], first[1][h]], axis=1).astype(BF16) for h in range(2)]
    b = [row_form(last[0][h], last[1][h]).astype(BF16) for h in range(2)]
    both = product(a, b)
    lane = halves(row_form(both[:, :order], both[:, order:]))
    lane_out[0] = lane[0]
    lane_out[1] = lane[1]
    for out, g in zip(left_outs, (1, 2, 3, 5)):
        parts = window(g, False)
        for h in range(2):
            out[h] = complex_form(parts[0][h], parts[1][h]).astype(BF16)


def matrices(gates, wires, flips, middle, chunks):
    order = gates.shape[-1]
    shape = jax.ShapeDtypeStruct((2, 2 * order, 2 * order), BF16)
    return pl.pallas_call(
        functools.partial(matrices_kernel, middle, chunks),
        out_shape=[in_vmem(shape)] * 5,
        in_specs=[SMEM, SMEM, VMEM],
        out_specs=[VMEM] * 5,
        compiler_params=LIMIT,
        name="matrices",
    )(wires, flips, gates)


def runs(slots):
    merged = []
    for at, (piece, place) in enumerate(slots):
        if merged and merged[-1][0] == piece and merged[-1][1] + merged[-1][3] == place:
            merged[-1][3] += 1
        else:
            merged.append([piece, place, at, 1])
    return merged


def stack(pieces, axis):
    return pieces[0] if len(pieces) == 1 else jnp.concatenate(pieces, axis=axis)


def left(matrix, loads):
    columns = jnp.concatenate([jnp.concatenate(pair, axis=0) for pair in loads], axis=1)
    out = product((matrix[0], matrix[1]), halves(columns))
    order = matrix.shape[-1] // 2
    return [
        (out[:order, k * order : (k + 1) * order], out[order:, k * order : (k + 1) * order])
        for k in range(len(loads))
    ]


def right(pairs, lane):
    order = lane.shape[-1] // 2
    rows = jnp.concatenate([jnp.concatenate(pair, axis=1) for pair in pairs], axis=0)
    rows = product(halves(rows), (lane[0], lane[1]))
    return [
        (rows[k * order : (k + 1) * order, :order], rows[k * order : (k + 1) * order, order:])
        for k in range(len(pairs))
    ]


def top_gate(matrix, chunk, sources, in_slots, targets, out_slots):
    order = matrix.shape[-1] // 2
    step = 2 * chunk
    per = min(2, chunk)

    def span(height, place, count, m, part):
        return pl.ds(place * height * step + 2 * m + part, count * height, stride=step)

    def body(i, carry):
        ms = [per * i + k for k in range(per)]
        tall = order // len(in_slots)
        loads = [
            tuple(
                stack([sources[o][span(tall, p, n, m, part), :] for o, p, _, n in runs(in_slots)], 0)
                for part in range(2)
            )
            for m in ms
        ]
        tall = order // len(out_slots)
        for m, pair in zip(ms, left(matrix, loads)):
            for part in range(2):
                for o, p, at, n in runs(out_slots):
                    targets[o][span(tall, p, n, m, part), :] = pair[part][at * tall : (at + n) * tall]
        return carry

    lax.fori_loop(0, chunk // per, body, 0)


def top_kernel(chunk, in_slots, out_slots, count, matrix, *refs):
    top_gate(matrix, chunk, refs[:count], in_slots, refs[count:], out_slots)


def final_kernel(chunk, in_slots, count, at, matrix, *refs):
    sources, out, scratch, semaphore = refs[:count], refs[-3], refs[-2], refs[-1]
    top_gate(matrix, chunk, sources, in_slots, [scratch], [(0, 0)])
    order = matrix.shape[-1] // 2
    copy = pltpu.make_async_copy(
        scratch.reshape(order, 2 * chunk, scratch.shape[-1]),
        out.at[:, pl.ds(2 * chunk * at, 2 * chunk), :],
        semaphore,
    )
    copy.start()
    copy.wait()


def inner_kernel(chunk, low, groups, matrix, lane, *refs):
    half = len(refs) // 2
    chunks = half // groups
    rows = low * chunk
    for g in range(groups):
        sources = refs[g * chunks : (g + 1) * chunks]
        targets = refs[half + g * chunks : half + (g + 1) * chunks]
        blocks = sources[0].shape[0] // (2 * rows)
        per = min(2, blocks)

        def body(k, carry, sources=sources, targets=targets, per=per):
            starts = [pl.multiple_of((per * k + q) * 2 * rows, 2 * rows) for q in range(per)]
            loads = [
                tuple(
                    stack([s[pl.ds(start + part, rows, stride=2), :] for s in sources], 0)
                    for part in range(2)
                )
                for start in starts
            ]
            for start, pair in zip(starts, right(left(matrix, loads), lane)):
                for part in range(2):
                    for c, t in enumerate(targets):
                        t[pl.ds(start + part, rows, stride=2), :] = pair[part][c * rows : (c + 1) * rows]
            return carry

        lax.fori_loop(0, blocks // per, body, 0)


def call(kernel, name, mats, sources, out_rows, lanes):
    return [
        keep(out)
        for out in pl.pallas_call(
            kernel,
            out_shape=[pltpu.VMEM((rows, lanes), F32) for rows in out_rows],
            in_specs=[VMEM] * (len(mats) + len(sources)),
            out_specs=[VMEM] * len(out_rows),
            compiler_params=LIMIT,
            name=name,
        )(*mats, *sources)
    ]


def split_by(bit, count):
    slots, filled = [], [0, 0]
    for s in range(count):
        side = s >> bit & 1
        slots.append((side, filled[side]))
        filled[side] += 1
    return slots


def gather_kernel(height, moves, *refs):
    for o, p, at, n in moves:
        refs[-1][pl.ds(at * height, n * height), :] = refs[o][pl.ds(p * height, n * height), :]


def exchange(order, slots, pieces, height):
    slots, pieces = list(slots), list(pieces)
    for step, (axis, bit, slot_bit) in enumerate(order):
        leaving = [s for s in range(len(slots)) if s >> slot_bit & 1]
        if step == 0:
            send = pieces[1]
        else:
            moves = runs([slots[s] for s in leaving])
            used = sorted({o for o, _, _, _ in moves})
            send = pl.pallas_call(
                functools.partial(gather_kernel, height, [(used.index(o), p, at, n) for o, p, at, n in moves]),
                out_shape=pltpu.VMEM((len(leaving) * height, pieces[0].shape[1]), F32),
                in_specs=[VMEM] * len(used),
                out_specs=VMEM,
                compiler_params=LIMIT,
                name="gather",
            )(*[pieces[o] for o in used])
        pairs = [(i, i ^ (1 << bit)) for i in range(lax.axis_size(axis))]
        pieces.append(keep(lax.ppermute(send, axis, pairs)))
        for at, s in enumerate(leaving):
            slots[s] = (len(pieces) - 1, at)
    used = sorted({o for o, _ in slots})
    return [(used.index(o), p) for o, p in slots], [pieces[o] for o in used]


def pack_kernel(chunk, at, slots, own, source, *refs):
    targets, semaphores = refs[:2], refs[2]
    copies = [
        pltpu.make_async_copy(
            source.at[jnp.bitwise_xor(own[0], s), :, pl.ds(2 * chunk * at, 2 * chunk), :],
            targets[o].at[p],
            semaphores.at[s],
        )
        for s, (o, p) in enumerate(slots)
    ]
    for copy in copies:
        copy.start()
    for copy in copies:
        copy.wait()


def pack(own, source, chunk, at, slots):
    count, height, _, lanes = source.shape
    shape = (count // 2, height, 2 * chunk, lanes)
    outs = pl.pallas_call(
        functools.partial(pack_kernel, chunk, at, slots),
        out_shape=[pltpu.VMEM(shape, F32)] * 2,
        in_specs=[SMEM, ANY],
        out_specs=[VMEM] * 2,
        scratch_shapes=[pltpu.SemaphoreType.DMA((count,))],
        compiler_params=LIMIT,
        name="pack",
    )(own, source)
    return [keep(out.reshape(-1, lanes)) for out in outs]


def rotate(order, by):
    by %= len(order)
    return order[by:] + order[:by]


def shards(amplitudes, gates, gate_wires):
    count = amplitudes.shape[1]
    order = gates.shape[-1]
    middle = count // (order * order)
    low = order // middle
    chunk = 4
    chunks = middle // chunk
    top = bits_of(order)
    nx, ny, nz = (bits_of(lax.axis_size(a)) for a in ("gx", "gy", "gz"))
    assert nx < top - bits_of(low)

    at_x, at_z = lax.axis_index("gx"), lax.axis_index("gz")
    at_yz = lax.axis_index("gy") * lax.axis_size("gz") + at_z
    in_1 = jnp.left_shift(at_yz, top - ny - nz)
    by_x = jnp.left_shift(at_x, top - nx)
    by_z = jnp.left_shift(at_z, top - nz)
    zero = jnp.zeros_like(by_x)
    flips = jnp.stack([zero, zero, by_x, in_1, zero, zero, by_z, by_x, zero, zero, zero, by_z])
    lane, m1, m2, m3, m5 = [keep(m) for m in matrices(gates, gate_wires, flips.reshape(6, 2), middle, chunks)]

    slots_1, slots_2, slots_3 = 1 << (ny + nz), 1 << nx, 1 << nz
    links = [("gz", b, b) for b in reversed(range(1, nz))] + [("gy", b, nz + b) for b in range(ny)]
    links = links[-1:] + links[:-1]
    near = [("gz", 0, 0)]
    links_3 = [("gz", b, b) for b in reversed(range(1, nz))]
    links_2 = [("gx", b, b) for b in reversed(range(nx))]

    rows = amplitudes.reshape(2, count // order, order)
    rows = with_layout_constraint(rows, Layout((1, 0, 2)))
    source = rows.transpose(1, 0, 2).reshape(slots_1, order // slots_1, 2 * middle, order)

    def rows_of(share):
        return order * 2 * chunk // share

    packed = []
    for c in range(chunks):
        steps = rotate(links, c) + near
        slots = split_by(steps[0][2], slots_1)
        packed.append((steps, slots, pack(at_yz.reshape(1), source, chunk, c, slots)))
    first = []
    out_slots = []
    for s in range(slots_2):
        side, place = divmod(s, slots_2 // 2)
        out_slots += [(side, place), (2 + side, place)]
    for c in range(chunks):
        steps, slots, pieces = packed[c]
        slots, pieces = exchange(steps, slots, pieces, rows_of(slots_1))
        first.append(
            call(
                functools.partial(top_kernel, chunk, slots, out_slots, len(pieces)),
                "first", (m1,), pieces, [rows_of(4)] * 4, order,
            )
        )

    def cross(stays, leaves):
        slots = [divmod(s, slots_2 // 2) for s in range(slots_2)]
        return exchange(links_2, slots, [stays, leaves], rows_of(2 * slots_2))

    def inner(groups, name):
        flat = [piece for group in groups for piece in group]
        outs = call(
            functools.partial(inner_kernel, chunk, low, len(groups)),
            name, (m2, lane), flat, [piece.shape[0] for piece in flat], order,
        )
        return [outs[g * chunks : (g + 1) * chunks] for g in range(len(groups))]

    early = [cross(p[0], p[1]) for p in first]
    late = inner([[p[2] for p in first], [p[3] for p in first]], "inner_late")
    early_slots = early[0][0]
    moved = inner([[e[1][k] for e in early] for k in range(len(early[0][1]))], "inner_early")
    crossed = [cross(late[0][c], late[1][c]) for c in range(chunks)]

    result = None
    for c in range(chunks):
        pieces = [group[c] for group in moved]
        in_slots = []
        for s in range(slots_2):
            o, p = crossed[c][0][s]
            in_slots += [early_slots[s], (len(pieces) + o, p)]
        pieces = pieces + crossed[c][1]
        steps = rotate(links_3, c) + near
        slots = split_by(steps[0][2], slots_3)
        pieces = call(
            functools.partial(top_kernel, chunk, in_slots, slots, len(pieces)),
            "third", (m3,), pieces, [rows_of(2)] * 2, order,
        )
        slots, pieces = exchange(steps, slots, pieces, rows_of(slots_3))
        extra = [] if result is None else [result]
        result = pl.pallas_call(
            functools.partial(final_kernel, chunk, slots, len(pieces), c),
            out_shape=jax.ShapeDtypeStruct((order, 2 * middle, order), F32),
            in_specs=[VMEM] * (1 + len(pieces)) + [ANY] * len(extra),
            out_specs=ANY,
            scratch_shapes=[pltpu.VMEM((rows_of(1), order), F32), pltpu.SemaphoreType.DMA],
            input_output_aliases={1 + len(pieces): 0} if extra else {},
            compiler_params=LIMIT,
            name="last",
        )(m5, *pieces, *extra)
    return result.reshape(count // order, 2, order).transpose(1, 0, 2).reshape(2, count)


def solution(mesh):
    in_specs = (P(None, ("gx", "gy", "gz")), P(), P())
    out_specs = P(None, ("gx", "gy", "gz"))
    return jax.shard_map(shards, mesh=mesh, in_specs=in_specs, out_specs=out_specs, check_vma=False)
```

```python
import functools

import jax
import jax.numpy as jnp
from jax import lax
from jax.experimental import pallas as pl
from jax.experimental.pallas import tpu as pltpu
from jax.experimental.layout import Layout, with_layout_constraint
from jax.sharding import PartitionSpec as P

F32 = jnp.float32
BF16 = jnp.bfloat16
VMEM = pl.BlockSpec(memory_space=pltpu.VMEM)
ANY = pl.BlockSpec(memory_space=pl.ANY)
LIMIT = pltpu.CompilerParams(vmem_limit_bytes=20 << 20)
SMEM = pl.BlockSpec(memory_space=pltpu.SMEM)


def bits_of(size):
    count = size.bit_length() - 1
    assert size == 1 << count
    return count


def in_vmem(shape):
    return pltpu.VMEM(shape.shape, shape.dtype)


def keep(value):
    return pltpu.with_memory_space_constraint(value, pltpu.VMEM)


def halves(value):
    high = value.astype(BF16)
    return high, (value - high.astype(F32)).astype(BF16)


def dot(a, b):
    return jnp.dot(a, b, preferred_element_type=F32)


def product(left, right):
    return dot(left[0], right[0]) + (dot(left[0], right[1]) + dot(left[1], right[0]))


def complex_form(real, imag):
    return jnp.concatenate(
        [jnp.concatenate([real, -imag], axis=1), jnp.concatenate([imag, real], axis=1)], axis=0
    )


def row_form(real, imag):
    return jnp.concatenate(
        [jnp.concatenate([real, imag], axis=1), jnp.concatenate([-imag, real], axis=1)], axis=0
    )


def matrices_kernel(middle, chunks, shifts, wires, own_x, own_yz, own_z, gates, lane_out, *left_outs):
    order = gates.shape[-1]
    width = wires.shape[1]
    by_x, by_yz, by_z = (
        jnp.left_shift(own[0], shift) for own, shift in zip((own_x, own_yz, own_z), shifts)
    )
    flips = {0: (0, 0), 1: (by_x, by_yz), 2: (0, 0), 3: (by_z, by_x), 4: (0, 0), 5: (0, by_z)}
    rows = lax.broadcasted_iota(jnp.int32, (order, order), 0)
    columns = lax.broadcasted_iota(jnp.int32, (order, order), 1)

    def picker(g, flip):
        index = jnp.bitwise_xor(rows, flip)
        if g == 2:
            rest = bits_of(middle // chunks)
            low = bits_of(order // middle)
            index = (
                jnp.left_shift(jnp.bitwise_and(jnp.right_shift(rows, rest), (1 << low) - 1), bits_of(middle))
                + jnp.left_shift(jnp.right_shift(rows, rest + low), rest)
                + jnp.bitwise_and(rows, (1 << rest) - 1)
            )
        mapped = jnp.zeros_like(index)
        for j in range(width):
            bit = jnp.bitwise_and(jnp.right_shift(index, j), 1)
            mapped = mapped + jnp.left_shift(bit, wires[g, j])
        return jnp.where(mapped == columns, 1.0, 0.0).astype(BF16)

    def window(g, transposed):
        row_pick = picker(g, flips[g][0])
        column_pick = picker(g, flips[g][1])
        parts = []
        for c in range(2):
            pair = []
            for half in halves(gates[g, c]):
                first = dot(row_pick, half).astype(BF16)
                a, b = (column_pick, first) if transposed else (first, column_pick)
                pair.append(
                    lax.dot_general(a, b, (((1,), (1,)), ((), ())), preferred_element_type=F32)
                )
            parts.append(pair)
        return parts

    first, last = window(0, True), window(4, True)
    a = [jnp.concatenate([first[0][h], first[1][h]], axis=1).astype(BF16) for h in range(2)]
    b = [row_form(last[0][h], last[1][h]).astype(BF16) for h in range(2)]
    both = product(a, b)
    lane = halves(row_form(both[:, :order], both[:, order:]))
    lane_out[0] = lane[0]
    lane_out[1] = lane[1]
    for out, g in zip(left_outs, (1, 2, 3, 5)):
        parts = window(g, False)
        for h in range(2):
            out[h] = complex_form(parts[0][h], parts[1][h]).astype(BF16)


def matrices(gates, wires, own, shifts, middle, chunks):
    order = gates.shape[-1]
    shape = jax.ShapeDtypeStruct((2, 2 * order, 2 * order), BF16)
    return pl.pallas_call(
        functools.partial(matrices_kernel, middle, chunks, shifts),
        out_shape=[in_vmem(shape)] * 5,
        in_specs=[SMEM] * 4 + [VMEM],
        out_specs=[VMEM] * 5,
        compiler_params=LIMIT,
        name="matrices",
    )(wires, *own, gates)


def runs(slots):
    merged = []
    for at, (piece, place) in enumerate(slots):
        if merged and merged[-1][0] == piece and merged[-1][1] + merged[-1][3] == place:
            merged[-1][3] += 1
        else:
            merged.append([piece, place, at, 1])
    return merged


def stack(pieces, axis):
    return pieces[0] if len(pieces) == 1 else jnp.concatenate(pieces, axis=axis)


def left(matrix, loads):
    columns = jnp.concatenate([jnp.concatenate(pair, axis=0) for pair in loads], axis=1)
    out = product((matrix[0], matrix[1]), halves(columns))
    order = matrix.shape[-1] // 2
    return [
        (out[:order, k * order : (k + 1) * order], out[order:, k * order : (k + 1) * order])
        for k in range(len(loads))
    ]


def right(pairs, lane):
    order = lane.shape[-1] // 2
    rows = jnp.concatenate([jnp.concatenate(pair, axis=1) for pair in pairs], axis=0)
    rows = product(halves(rows), (lane[0], lane[1]))
    return [
        (rows[k * order : (k + 1) * order, :order], rows[k * order : (k + 1) * order, order:])
        for k in range(len(pairs))
    ]


def top_gate(matrix, chunk, sources, in_slots, targets, out_slots):
    order = matrix.shape[-1] // 2
    step = 2 * chunk
    per = min(2, chunk)

    def span(height, place, count, m, part):
        return pl.ds(place * height * step + 2 * m + part, count * height, stride=step)

    def body(i, carry):
        ms = [per * i + k for k in range(per)]
        tall = order // len(in_slots)
        loads = [
            tuple(
                stack([sources[o][span(tall, p, n, m, part), :] for o, p, _, n in runs(in_slots)], 0)
                for part in range(2)
            )
            for m in ms
        ]
        tall = order // len(out_slots)
        for m, pair in zip(ms, left(matrix, loads)):
            for part in range(2):
                for o, p, at, n in runs(out_slots):
                    targets[o][span(tall, p, n, m, part), :] = pair[part][at * tall : (at + n) * tall]
        return carry

    lax.fori_loop(0, chunk // per, body, 0)


def top_kernel(chunk, in_slots, out_slots, count, matrix, *refs):
    top_gate(matrix, chunk, refs[:count], in_slots, refs[count:], out_slots)


def final_kernel(chunk, in_slots, count, at, matrix, *refs):
    sources, out, scratch, semaphore = refs[:count], refs[-3], refs[-2], refs[-1]
    top_gate(matrix, chunk, sources, in_slots, [scratch], [(0, 0)])
    order = matrix.shape[-1] // 2
    copy = pltpu.make_async_copy(
        scratch.reshape(order, 2 * chunk, scratch.shape[-1]),
        out.at[:, pl.ds(2 * chunk * at, 2 * chunk), :],
        semaphore,
    )
    copy.start()
    copy.wait()


def inner_kernel(chunk, low, groups, matrix, lane, *refs):
    half = len(refs) // 2
    chunks = half // groups
    rows = low * chunk
    for g in range(groups):
        sources = refs[g * chunks : (g + 1) * chunks]
        targets = refs[half + g * chunks : half + (g + 1) * chunks]
        blocks = sources[0].shape[0] // (2 * rows)
        per = min(2, blocks)

        def body(k, carry, sources=sources, targets=targets, per=per):
            starts = [pl.multiple_of((per * k + q) * 2 * rows, 2 * rows) for q in range(per)]
            loads = [
                tuple(
                    stack([s[pl.ds(start + part, rows, stride=2), :] for s in sources], 0)
                    for part in range(2)
                )
                for start in starts
            ]
            for start, pair in zip(starts, right(left(matrix, loads), lane)):
                for part in range(2):
                    for c, t in enumerate(targets):
                        t[pl.ds(start + part, rows, stride=2), :] = pair[part][c * rows : (c + 1) * rows]
            return carry

        lax.fori_loop(0, blocks // per, body, 0)


def call(kernel, name, mats, sources, out_rows, lanes):
    return [
        keep(out)
        for out in pl.pallas_call(
            kernel,
            out_shape=[pltpu.VMEM((rows, lanes), F32) for rows in out_rows],
            in_specs=[VMEM] * (len(mats) + len(sources)),
            out_specs=[VMEM] * len(out_rows),
            compiler_params=LIMIT,
            name=name,
        )(*mats, *sources)
    ]


def split_by(bits, count):
    slots, filled = [], [0] * (1 << len(bits))
    for s in range(count):
        piece = sum((s >> bit[2] & 1) << k for k, bit in enumerate(bits))
        slots.append((piece, filled[piece]))
        filled[piece] += 1
    return slots


def gather_kernel(height, moves, *refs):
    for o, p, at, n in moves:
        refs[-1][pl.ds(at * height, n * height), :] = refs[o][pl.ds(p * height, n * height), :]


def after(value, *others):
    return lax.optimization_barrier((value, others))[0]


def gather(pieces, slots, leaving, height):
    moves = runs([slots[s] for s in leaving])
    used = sorted({o for o, _, _, _ in moves})
    if len(moves) == 1 and moves[0][3] * height == pieces[used[0]].shape[0]:
        return pieces[used[0]]
    return pl.pallas_call(
        functools.partial(gather_kernel, height, [(used.index(o), p, at, n) for o, p, at, n in moves]),
        out_shape=pltpu.VMEM((len(leaving) * height, pieces[0].shape[1]), F32),
        in_specs=[VMEM] * len(used),
        out_specs=VMEM,
        compiler_params=LIMIT,
        name="gather",
    )(*[pieces[o] for o in used])


def exchange_round(bits, slots, pieces, height):
    slots, pieces = list(slots), list(pieces)
    axis = bits[0][0]
    place = {}
    for mask in range(1, 1 << len(bits)):
        chosen = [k for k in range(len(bits)) if mask >> k & 1]
        far = sum(1 << bits[k][1] for k in chosen)
        leaving = [
            s
            for s in range(len(slots))
            if all((s >> bits[k][2] & 1) == (mask >> k & 1) for k in range(len(bits)))
        ]
        send = gather(pieces, slots, leaving, height)
        pairs = [(i, i ^ far) for i in range(lax.axis_size(axis))]
        pieces.append(keep(lax.ppermute(send, axis, pairs)))
        for at, s in enumerate(leaving):
            place[s] = (len(pieces) - 1, at)
    return [place.get(s, slots[s]) for s in range(len(slots))], pieces


def compact(slots, pieces):
    used = sorted({o for o, _ in slots})
    return [(used.index(o), p) for o, p in slots], [pieces[o] for o in used]


def exchange(rounds, slots, pieces, height):
    for bits in rounds:
        slots, pieces = exchange_round(bits, slots, pieces, height)
    return compact(slots, pieces)


def pack_kernel(chunk, at, slots, own, source, *refs):
    targets, semaphores = refs[:-1], refs[-1]
    copies = [
        pltpu.make_async_copy(
            source.at[jnp.bitwise_xor(own[0], s), :, pl.ds(2 * chunk * at, 2 * chunk), :],
            targets[o].at[p],
            semaphores.at[s],
        )
        for s, (o, p) in enumerate(slots)
    ]
    for copy in copies:
        copy.start()
    for copy in copies:
        copy.wait()


def pack(own, source, chunk, at, slots):
    count, height, _, lanes = source.shape
    parts = 1 + max(o for o, _ in slots)
    shape = (count // parts, height, 2 * chunk, lanes)
    outs = pl.pallas_call(
        functools.partial(pack_kernel, chunk, at, slots),
        out_shape=[pltpu.VMEM(shape, F32)] * parts,
        in_specs=[SMEM, ANY],
        out_specs=[VMEM] * parts,
        scratch_shapes=[pltpu.SemaphoreType.DMA((count,))],
        compiler_params=LIMIT,
        name="pack",
    )(own, source)
    return [keep(out.reshape(-1, lanes)) for out in outs]


def shards(amplitudes, gates, gate_wires):
    count = amplitudes.shape[1]
    order = gates.shape[-1]
    middle = count // (order * order)
    low = order // middle
    chunk = 4
    chunks = middle // chunk
    top = bits_of(order)
    nx, ny, nz = (bits_of(lax.axis_size(a)) for a in ("gx", "gy", "gz"))
    assert nx < top - bits_of(low)

    at_x, at_z = lax.axis_index("gx"), lax.axis_index("gz")
    at_yz = lax.axis_index("gy") * lax.axis_size("gz") + at_z
    own = [index.reshape(1) for index in (at_x, at_yz, at_z)]
    mats = matrices(gates, gate_wires, own, (top - nx, top - ny - nz, top - nz), middle, chunks)
    lane, m1, m2, m3, m5 = [keep(m) for m in mats]

    slots_1, slots_2, slots_3 = 1 << (ny + nz), 1 << nx, 1 << nz
    outer = [[("gy", b, nz + b)] for b in reversed(range(ny))]
    inner_bits = [("gz", b, b) for b in reversed(range(1, nz))]
    plane = [inner_bits[k : k + 2] for k in range(0, len(inner_bits), 2)]
    near = [[("gz", 0, 0)]]
    across = [[("gx", b, b)] for b in reversed(range(nx))]

    rows = amplitudes.reshape(2, count // order, order)
    rows = with_layout_constraint(rows, Layout((1, 0, 2)))
    source = rows.transpose(1, 0, 2).reshape(slots_1, order // slots_1, 2 * middle, order)
    source = pltpu.with_memory_space_constraint(source, pltpu.HBM)

    def rows_of(share):
        return order * 2 * chunk // share

    out_slots = []
    for s in range(slots_2):
        side, place = divmod(s, slots_2 // 2)
        out_slots += [(side, place), (2 + side, place)]

    def begin(c, source):
        rounds = (outer + plane if c % 2 == 0 else plane + outer) + near
        slots = split_by(rounds[0], slots_1)
        pieces = pack(own[1], source, chunk, c, slots)
        slots, pieces = exchange_round(rounds[0], slots, pieces, rows_of(slots_1))
        return rounds[1:], slots, pieces

    begun = [begin(0, source), begin(1, source)]
    mark = begun[0][2][-1]
    mark, m1, m2, m3, m5, lane = lax.optimization_barrier((mark, m1, m2, m3, m5, lane))
    begun[0][2][-1] = mark
    source = after(source, mark)
    begun += [begin(c, source) for c in range(2, chunks)]
    first = []
    for rounds, slots, pieces in begun:
        slots, pieces = exchange(rounds, slots, pieces, rows_of(slots_1))
        first.append(
            call(
                functools.partial(top_kernel, chunk, slots, out_slots, len(pieces)),
                "first", (m1,), pieces, [rows_of(4)] * 4, order,
            )
        )

    def cross(stays, leaves):
        slots = [divmod(s, slots_2 // 2) for s in range(slots_2)]
        return exchange(across, slots, [stays, leaves], rows_of(2 * slots_2))

    def inner(groups, name):
        flat = [piece for group in groups for piece in group]
        outs = call(
            functools.partial(inner_kernel, chunk, low, len(groups)),
            name, (m2, lane), flat, [piece.shape[0] for piece in flat], order,
        )
        return [outs[g * chunks : (g + 1) * chunks] for g in range(len(groups))]

    early = [cross(p[0], p[1]) for p in first]
    late = inner([[p[2] for p in first], [p[3] for p in first]], "inner_late")
    early_slots = early[0][0]
    moved = inner([[e[1][k] for e in early] for k in range(len(early[0][1]))], "inner_early")
    crossed = [cross(late[0][c], late[1][c]) for c in range(chunks)]

    result = None
    for c in range(chunks):
        pieces = [group[c] for group in moved]
        in_slots = []
        for s in range(slots_2):
            o, p = crossed[c][0][s]
            in_slots += [early_slots[s], (len(pieces) + o, p)]
        pieces = pieces + crossed[c][1]
        steps = plane + near
        slots = split_by(steps[0], slots_3)
        pieces = call(
            functools.partial(top_kernel, chunk, in_slots, slots, len(pieces)),
            "third", (m3,), pieces, [rows_of(1 << len(steps[0]))] * (1 << len(steps[0])), order,
        )
        slots, pieces = exchange(steps, slots, pieces, rows_of(slots_3))
        extra = [] if result is None else [result]
        result = pl.pallas_call(
            functools.partial(final_kernel, chunk, slots, len(pieces), c),
            out_shape=jax.ShapeDtypeStruct((order, 2 * middle, order), F32),
            in_specs=[VMEM] * (1 + len(pieces)) + [ANY] * len(extra),
            out_specs=ANY,
            scratch_shapes=[pltpu.VMEM((rows_of(1), order), F32), pltpu.SemaphoreType.DMA],
            input_output_aliases={1 + len(pieces): 0} if extra else {},
            compiler_params=LIMIT,
            name="last",
        )(m5, *pieces, *extra)
    return result.reshape(count // order, 2, order).transpose(1, 0, 2).reshape(2, count)


def solution(mesh):
    in_specs = (P(None, ("gx", "gy", "gz")), P(), P())
    out_specs = P(None, ("gx", "gy", "gz"))
    return jax.shard_map(shards, mesh=mesh, in_specs=in_specs, out_specs=out_specs, check_vma=False)
```
